256 devices in a mesh: scen: 64 (over y, z, core), link: 4 (over x).
Axes of the slice: x: 4, y: 4, z: 8, core: 2. Of those that a mesh axis runs over, the one named last changes fastest.
Arguments:
- factor_inv: bfloat16 [128, 1024, 1024], P('scen'), may hold values from -0.1875 to 0.1875
- coupling: bfloat16 [128, 1024, 1024], P('scen', None, 'link'), may hold values from -0.375 to 0.375
- first_diag: float32 [128, 128], P('scen'), may hold values from 1 to 10
- pattern: int32 [128, 8], P('scen'), may hold values from 0 to 127, as said below
Outputs:
- panel: float32 [16384, 128], P('scen')
- trailing: float32 [16384, 16384], P('scen', 'link')
The draws below stay inside these ranges and needn't reach their ends.
Inputs may be any that keep to these rules, and one draw needn't show every extreme that they name: `pattern`: slot t of a scenario names a block of column range t // 2, that is, a block p with p // 32 = t // 2. The 2 scenarios of rows s * 2 to (s + 1) * 2 - 1 name every block at most once among them, and at most 1 block of any one group of blocks with the same p // 2. The first scenario of every such set names block 0 in slot 0.
All inputs are finite; a program needn't handle non-finite values.
Results may differ from the reference program's by a relative error of at most 0.0005.
Values may be sent and summed in bfloat16 or wider, within the bound.
No kernel may reach another device: no remote copies, remote signals or barrier semaphores. Data moves between devices by JAX's collectives and lax.ppermute only.
A program may use at most 128 MiB of HBM per device.

```python
import math
import jax
import jax.numpy as jnp
from jax import lax

NB = 128
TILE = 128
NS = 1024
KL = 2
S_DEV = 2
KB = 8
SCENARIOS = 128
N_SCEN = 64
N_LINK = 4


def draw_pattern(key, part):
    per_range = NB // N_LINK
    owner_rows = NB // N_SCEN
    picks = S_DEV * KL
    owners_here = per_range // owner_rows
    limit = max(1, (picks + owners_here - 1) // owners_here)
    key_pop, key_noise = jax.random.split(jax.random.fold_in(key, 7))
    popular = jax.random.randint(key_pop, (N_LINK, per_range), 0, 4)
    noise = jax.random.randint(key_noise, (N_SCEN, N_LINK, per_range), 0, 65536)
    position = lax.broadcasted_iota(jnp.int32, (N_SCEN, N_LINK, per_range), 2)
    range_pos = lax.broadcasted_iota(jnp.int32, (N_SCEN, N_LINK, per_range), 1)
    leading = ((position == 0) & (range_pos == 0)).astype(jnp.int32) * 16777216
    scores = (popular[None, :, :] * 65536 + noise) * per_range + position + leading
    grouped = scores.reshape(N_SCEN, N_LINK, owners_here, owner_rows)
    above = jnp.sum((grouped[:, :, :, None, :] > grouped[:, :, :, :, None]).astype(jnp.int32), axis=4)
    allowed = (above < limit).astype(jnp.int32).reshape(N_SCEN, N_LINK, per_range)
    final = allowed * 67108864 + scores
    order = jnp.argsort(-final, axis=2, stable=True)
    chosen = order[:, :, :picks].reshape(N_SCEN, N_LINK, S_DEV, KL).transpose(0, 2, 1, 3)
    offsets = (jnp.arange(N_LINK, dtype=jnp.int32) * per_range)[None, None, :, None]
    return (chosen + offsets).reshape(N_SCEN * S_DEV, N_LINK * KL).astype(jnp.int32)


def draw_coupling(key, part):
    key_own, key_common = jax.random.split(jax.random.fold_in(key, 11))
    own = jnp.clip(jax.random.normal(key_own, (SCENARIOS, NS, KB * TILE), jnp.float32), -6.0, 6.0)
    common = jnp.clip(jax.random.normal(key_common, (SCENARIOS, NS, 1), jnp.float32), -6.0, 6.0)
    return ((own + common) * NS ** (-0.5)).astype(jnp.bfloat16)


def levels(key, dims, shards, smallest, high):
    gain, own = 1.0, jax.random.fold_in(key, 6)
    for dim, parts in shards:
        heights = jnp.exp(jax.random.uniform(jax.random.fold_in(own, dim), (parts,), jnp.float32, smallest / len(shards), high / len(shards)))
        gain = gain * jnp.repeat(heights, dims[dim] // parts).reshape([-1 if axis == dim else 1 for axis in range(len(dims))])
    return gain


def scatter_about(stream_key, dims, scale, reach, shards=(), held_as=jnp.bfloat16):
    factor_of = levels(stream_key, dims, shards, -0.22, 0.18) if shards else 1.0
    entries = jax.random.normal(stream_key, dims, jnp.float32) * scale * factor_of
    return jnp.minimum(jnp.maximum(entries, -reach), reach).astype(held_as)


def setup_inputs(seed: int = 0) -> dict:
    splits = jax.random.split(jax.random.key(seed), 5)
    return {
        "factor_inv": scatter_about(splits[0], (SCENARIOS, NS, NS), NS ** -0.5, 0.1875, ((0, 64),)),
        "coupling": draw_coupling(jax.random.fold_in(splits[4], 71), 0),
        "first_diag": jnp.clip(jnp.exp(math.log(10.0) - 2.3025851 * jax.random.uniform(splits[2], (NB, TILE), jnp.float32) ** levels(splits[2], (NB, TILE), ((0, 64),), -0.2, 0.2)), 1.0, 10.0),
        "pattern": draw_pattern(jax.random.fold_in(splits[4], 71), 0),
    }


def reference(factor_inv, coupling, first_diag, pattern):

    def add_scenario(tiles, inputs):
        factor, columns, picked = inputs
        slabs = jnp.dot(factor.astype(jnp.float32), columns.astype(jnp.float32), preferred_element_type=jnp.float32).astype(jnp.bfloat16)
        gram = jnp.dot(slabs.T.astype(jnp.float32), slabs.astype(jnp.float32), preferred_element_type=jnp.float32)
        gram_tiles = gram.reshape(KB, TILE, KB, TILE).transpose(0, 2, 1, 3)
        picked = picked.astype(jnp.int32)
        return (tiles.at[picked[:, None], picked[None, :]].add(gram_tiles), None)
    empty = jnp.zeros((NB, NB, TILE, TILE), jnp.float32)
    tiles, unused = lax.scan(add_scenario, empty, (factor_inv, coupling, pattern))
    diag_tiles = first_diag[:, :, None] * jnp.eye(TILE, dtype=jnp.float32)[None, :, :]
    span = jnp.arange(NB, dtype=jnp.int32)
    tiles = tiles.at[span, span].add(diag_tiles)
    schur = tiles.transpose(0, 2, 1, 3).reshape(NB * TILE, NB * TILE)
    lead_factor = jnp.linalg.cholesky(schur[:TILE, :TILE])
    solved = jax.scipy.linalg.solve_triangular(lead_factor, schur[:, :TILE].T, lower=True).T
    panel = jnp.concatenate([lead_factor, solved[TILE:]], axis=0)
    trailing = schur - jnp.dot(panel.astype(jnp.float32), panel.T.astype(jnp.float32), precision=lax.Precision.HIGHEST, preferred_element_type=jnp.float32)
    return (panel, trailing)
```

```python
import jax
import jax.numpy as jnp
from jax import lax
from jax.experimental import pallas as pl
from jax.experimental.pallas import tpu as pltpu
from jax.sharding import Mesh, PartitionSpec as P

SCALE = 2.0**-7
HIGH = lax.Precision.HIGHEST
TILE = 128
PER_STEP = 4


def ring(count, shift):
    return [(i, (i + shift) % count) for i in range(count)]


def shifted(value, axis, count, shift):
    return lax.ppermute(value, axis, ring(count, shift))


def after(value, *others):
    return lax.optimization_barrier((value,) + others)[0]


def gather_relative(value, axis, count):
    return jnp.stack([value] + [shifted(value, axis, count, k) for k in range(1, count)])


def gather_ring4(value, axis):
    half = value.shape[0] // 2
    low = shifted(value, axis, 4, 1)
    high = shifted(value, axis, 4, -1)
    across = jnp.concatenate(
        [shifted(low[:half], axis, 4, 1), shifted(high[half:], axis, 4, -1)], axis=0
    )
    return [value, low, across, high]


def gather_ring8(value, axis):
    half = value.shape[0] // 2
    got = [value] + [None] * 7
    low = high = value
    for k in range(1, 4):
        low = shifted(low, axis, 8, 1)
        high = shifted(high, axis, 8, -1)
        got[k], got[8 - k] = low, high
    got[4] = jnp.concatenate(
        [shifted(low[:half], axis, 8, 1), shifted(high[half:], axis, 8, -1)], axis=0
    )
    return got


def add_tiles(table, tiles, out):
    step = pl.program_id(0)
    for i in range(PER_STEP):
        source = step * PER_STEP + i

        @pl.when(table[0, source] > 0)
        def _():
            row = pl.multiple_of(table[1, source] * TILE, TILE)
            for t in range(2):
                col = pl.multiple_of(table[2 + t, source] * TILE, TILE)
                out[pl.ds(row, TILE), pl.ds(col, TILE)] += tiles[i, :, t * TILE : (t + 1) * TILE]


def first_kernel(table, place, panel, parts, diag, tiles, out, rows):
    @pl.when(pl.program_id(0) == 0)
    def _():
        count = parts.shape[1]
        sub = parts.shape[2]
        for g in range(parts.shape[0]):
            for q in range(count):
                rows[q * TILE + g * sub : q * TILE + (g + 1) * sub, :] = parts[place[g], q]
        for q in range(0, count, 2):
            span = slice(q * TILE, (q + 2) * TILE)
            out[:, span] = -lax.dot_general(
                panel[...],
                rows[span, :],
                (((1,), (1,)), ((), ())),
                precision=HIGH,
                preferred_element_type=jnp.float32,
            )
        same = lax.broadcasted_iota(jnp.int32, (TILE, TILE), 0) == lax.broadcasted_iota(
            jnp.int32, (TILE, TILE), 1
        )

        @pl.when(place[8] >= 0)
        def _():
            for i in range(2):
                col = pl.multiple_of((jnp.maximum(place[8], 0) + i) * TILE, TILE)
                out[i * TILE : (i + 1) * TILE, pl.ds(col, TILE)] += jnp.where(
                    same, diag[i : i + 1, :], 0.0
                )

    add_tiles(table, tiles, out)


def second_kernel(table, start, tiles, out):
    @pl.when(pl.program_id(0) == 0)
    def _():
        out[...] = start[...]

    add_tiles(table, tiles, out)


def whole(shape):
    return pl.BlockSpec(shape, lambda i, *_: (0,) * len(shape))


def tile_spec(tiles):
    return pl.BlockSpec((PER_STEP,) + tiles.shape[1:], lambda i, *_: (i, 0, 0))


def first_sum(table, place, panel, parts, diag, tiles, shape):
    return pl.pallas_call(
        first_kernel,
        grid_spec=pltpu.PrefetchScalarGridSpec(
            num_scalar_prefetch=2,
            grid=(tiles.shape[0] // PER_STEP,),
            in_specs=[whole(panel.shape), whole(parts.shape), whole(diag.shape), tile_spec(tiles)],
            out_specs=whole(shape),
            scratch_shapes=[pltpu.VMEM((shape[1], TILE), jnp.float32)],
        ),
        out_shape=jax.ShapeDtypeStruct(shape, jnp.float32),
        name="first_sum",
    )(table, place, panel, parts, diag, tiles)


def second_sum(table, start, tiles):
    return pl.pallas_call(
        second_kernel,
        grid_spec=pltpu.PrefetchScalarGridSpec(
            num_scalar_prefetch=1,
            grid=(tiles.shape[0] // PER_STEP,),
            in_specs=[whole(start.shape), tile_spec(tiles)],
            out_specs=whole(start.shape),
        ),
        out_shape=jax.ShapeDtypeStruct(start.shape, jnp.float32),
        name="second_sum",
    )(table, start, tiles)


def per_device(factor_inv, coupling, first_diag, pattern):
    ny, nz, nc, nx = 4, 8, 2, 4
    yi, zi, ci, xi = (lax.axis_index(a) for a in ("y", "z", "c", "x"))
    here = (yi * nz + zi) * nc + ci
    per_range = 32
    f32 = jnp.float32

    names = gather_relative(pattern, "c", nc)
    names = gather_relative(names, "y", ny)
    names = gather_relative(names, "z", nz)

    def slabs_of(s):
        return jnp.dot(factor_inv[s], coupling[s], preferred_element_type=f32).astype(jnp.bfloat16)

    slab0 = slabs_of(0)
    slab1 = slabs_of(1)
    even = gather_ring4(slab0[:, :TILE], "x")
    odd = gather_ring4(slab0[:, TILE:], "x")
    late = gather_ring4(after(slab1, even[2]), "x")

    lead = jnp.where(xi == 0, even[0], jnp.where(xi == 1, even[1], jnp.where(xi == 2, even[2], even[3])))
    column = jnp.einsum("nr,nc->rc", slab0, lead, preferred_element_type=f32)
    corner = jnp.einsum("nr,nc->rc", lead, lead, preferred_element_type=f32)
    unit = jnp.eye(TILE, dtype=f32)
    corner = corner + jnp.where(here == 0, 1.0, 0.0) * (first_diag[0][:, None] * unit)
    parts = ny * nc
    sub = TILE // parts
    split = jnp.concatenate([column, corner], axis=0).reshape(3, parts, sub, TILE).transpose(1, 0, 2, 3)
    split = lax.all_to_all(split, ("y", "c"), 0, 0, tiled=True)
    corner_part = jnp.sum(split[:, 2], axis=0)
    packed = jnp.concatenate([split[:, :2].reshape(parts * 2 * sub, TILE), corner_part], axis=0)
    ringed = gather_ring8(packed, "z")
    packed = jnp.stack(ringed)
    corner_part = jnp.sum(packed[:, parts * 2 * sub :], axis=0)
    corner_pair = gather_relative(corner_part, "c", nc)
    corner_all = gather_relative(corner_pair, "y", ny)
    group = jnp.arange(parts)
    from_y = lax.rem(yi - group // nc + ny, ny)
    from_c = lax.rem(ci - group % nc + nc, nc)
    corner_sum = jnp.take(corner_all.reshape(parts, sub, TILE), from_y * nc + from_c, axis=0)
    corner_sum = corner_sum.reshape(TILE, TILE)

    def spread(made):
        stack = (jnp.stack(made) * SCALE).astype(jnp.float16).reshape(nx, 2, TILE, 2 * TILE)
        picks = [
            lax.dynamic_index_in_dim(stack, lax.rem(yi + m - xi + nx, nx), 0, keepdims=False)
            for m in range(ny)
        ]
        return jnp.stack([picks[0]] + [shifted(picks[m], "y", ny, m) for m in range(1, ny)])

    def product(block, slab):
        return jnp.einsum("nr,nc->rc", block, slab, preferred_element_type=f32)

    made0 = [
        jnp.stack([product(even[-j % nx], slab0), product(odd[-j % nx], slab0)]) for j in range(nx)
    ]
    made1 = [product(late[-j % nx], slab1) for j in range(nx)]
    bulk0 = gather_ring8(after(spread(made0), ringed[4]), "z")
    bulk1 = gather_ring8(after(spread(made1), ringed[4]), "z")

    chunks = packed[:, : parts * 2 * sub].reshape(nz * parts * 2, sub * TILE)
    firsts = lax.dynamic_slice_in_dim(names[:, :, :, 0], xi * 2, 2, 3) - xi * per_range
    firsts = jnp.take(firsts, lax.rem(yi - jnp.arange(ny) + ny, ny), axis=1)
    firsts = jnp.take(firsts, lax.rem(ci - jnp.arange(nc) + nc, nc), axis=2).reshape(-1)
    pick = (jnp.arange(per_range)[:, None] == firsts[None, :]).astype(f32)
    column_rows = jnp.dot(pick, chunks, precision=HIGH, preferred_element_type=f32)
    column_rows = column_rows.reshape(per_range * sub, TILE)
    factor = jnp.linalg.cholesky(corner_sum)
    factor = after(factor, bulk0[1], bulk0[7])
    solved = jax.scipy.linalg.solve_triangular(factor, column_rows.T, lower=True).T
    part = yi * nc + ci
    top = lax.dynamic_slice_in_dim(factor, part * sub, sub, 0)
    solved = jnp.concatenate([jnp.where(xi == 0, top, solved[:sub]), solved[sub:]], axis=0)
    solved = after(solved.reshape(per_range, sub, TILE), bulk1[1], bulk1[7])
    rows = jnp.stack(gather_ring4(solved, "y"))
    rows = jnp.stack([rows, shifted(rows, "c", nc, 1)], axis=1)
    rows = rows.reshape(parts, per_range, sub, TILE)
    own = lax.dynamic_slice_in_dim(rows, lax.rem(here, 16) * 2, 2, 1)
    own = jnp.take(own, from_y * nc + from_c, axis=0).transpose(1, 0, 2, 3).reshape(2 * TILE, TILE)
    panel = jnp.where(xi == yi, own, 0.0)
    for k in range(1, nx):
        panel = panel + lax.ppermute(
            own, ("y", "x"), [(r * nx + r, r * nx + (r + k) % nx) for r in range(ny)]
        )

    def matches(owner):
        mine = lax.dynamic_slice_in_dim(names, yi * 2, 2, 4)
        return mine // 2 == owner, mine % 2

    to_me, parity = matches(here)
    to_other, _ = matches(here + 1 - 2 * ci)
    cols = lax.dynamic_slice_in_dim(names, xi * 2, 2, 4) - xi * per_range
    hit = to_me.astype(jnp.int32)
    fields = jnp.stack(
        [
            jnp.sum(hit, axis=(3, 4)),
            jnp.sum(hit * parity, axis=(3, 4)),
            jnp.sum(jnp.sum(hit, axis=4) * cols[..., 0], axis=3),
            jnp.sum(jnp.sum(hit, axis=4) * cols[..., 1], axis=3),
        ]
    )
    fields = fields.transpose(0, 1, 3, 2)

    def choose(k, match):
        def flag(s, t):
            return match[k, :, 0, s, t][:, None, None]

        first, second = bulk0[k], bulk1[k]
        return jnp.where(
            flag(0, 0),
            first[:, 0],
            jnp.where(flag(0, 1), first[:, 1], jnp.where(flag(1, 0), second[:, 0], second[:, 1])),
        )

    def batch(ks):
        got = []
        for k in ks:
            got += [choose(k, to_me), shifted(choose(k, to_other), "c", nc, 1)]
        tiles = jnp.concatenate([g.astype(f32) * (1.0 / SCALE) for g in got], axis=0)
        return jnp.concatenate([fields[:, k] for k in ks], axis=1).reshape(4, -1), tiles

    first_table, first_tiles = batch((0, 1, 7, 2, 6))
    last_table, last_tiles = batch((3, 5, 4))
    at = here * 2 - xi * per_range
    at = jnp.where((at >= 0) & (at < per_range), at, -1)
    place = jnp.concatenate([from_y * nc + from_c, at[None]]).astype(jnp.int32)
    start = first_sum(
        first_table, place, panel, rows, first_diag, first_tiles, (2 * TILE, per_range * TILE)
    )
    return panel, second_sum(last_table, start, last_tiles)


def solution(mesh):
    grid = Mesh(mesh.devices.reshape(4, 8, 2, 4), ("y", "z", "c", "x"))
    scen = ("y", "z", "c")
    in_specs = (P(scen, None, None), P(scen, None, "x"), P(scen, None), P(scen, None))
    out_specs = (P(scen, None), P(scen, "x"))
    return jax.shard_map(
        per_device, mesh=grid, in_specs=in_specs, out_specs=out_specs, check_vma=False
    )
```

```python
import jax
import jax.numpy as jnp
from jax import lax
from jax.experimental import pallas as pl
from jax.experimental.pallas import tpu as pltpu
from jax.sharding import Mesh, PartitionSpec as P

SCALE = 2.0**-7
HIGH = lax.Precision.HIGHEST
TILE = 128
SPAN = 8


def ring(count, shift):
    return [(i, (i + shift) % count) for i in range(count)]


def shifted(value, axis, count, shift):
    return lax.ppermute(value, axis, ring(count, shift))


def after(value, *others):
    return lax.optimization_barrier((value,) + others)[0]


def copies(value, axis, count):
    return lax.all_to_all(
        jnp.broadcast_to(value[None], (count,) + value.shape), axis, 0, 0, tiled=True
    )


def gather_ring4(value, axis, *others):
    half = value.shape[0] // 2
    low = shifted(value, axis, 4, 1)
    high = shifted(value, axis, 4, -1)
    low, high = lax.optimization_barrier((low, high) + others)[:2]
    across = jnp.concatenate(
        [shifted(low[:half], axis, 4, 1), shifted(high[half:], axis, 4, -1)], axis=0
    )
    return [value, low, across, high]


def gather_ring8(value, axis):
    half = value.shape[0] // 2
    got = [value] + [None] * 7
    low = high = value
    for k in range(1, 4):
        low = shifted(low, axis, 8, 1)
        high = shifted(high, axis, 8, -1)
        got[k], got[8 - k] = low, high
    got[4] = jnp.concatenate(
        [shifted(low[:half], axis, 8, 1), shifted(high[half:], axis, 8, -1)], axis=0
    )
    return got


def add_tiles(table, tiles, out):
    first = pl.program_id(0) * SPAN

    def one(source, carry):
        row = pl.multiple_of(table[1, source] * TILE, TILE)
        for t in range(2):
            at = table[2 + t, source] - first

            @pl.when((table[0, source] > 0) & (at >= 0) & (at < SPAN))
            def _():
                col = pl.multiple_of(at * TILE, TILE)
                out[pl.ds(row, TILE), pl.ds(col, TILE)] += tiles[
                    source, :, t * TILE : (t + 1) * TILE
                ]

        return carry

    lax.fori_loop(0, tiles.shape[0], one, 0)


def first_kernel(table, place, weight, near, far, diag, tiles, out):
    half = near.shape[0]
    for q in range(0, SPAN, 2):
        span = slice(q * TILE, (q + 2) * TILE)
        out[:, span] = -sum(
            lax.dot_general(
                weight[i * half : (i + 1) * half, :],
                rows[:, span],
                (((0,), (0,)), ((), ())),
                precision=HIGH,
                preferred_element_type=jnp.float32,
            )
            for i, rows in enumerate((near, far))
        )
    same = lax.broadcasted_iota(jnp.int32, (TILE, TILE), 0) == lax.broadcasted_iota(
        jnp.int32, (TILE, TILE), 1
    )
    for i in range(2):
        at = place[0] + i - pl.program_id(0) * SPAN

        @pl.when((at >= 0) & (at < SPAN))
        def _():
            col = pl.multiple_of(at * TILE, TILE)
            out[i * TILE : (i + 1) * TILE, pl.ds(col, TILE)] += jnp.where(
                same, diag[i : i + 1, :], 0.0
            )

    add_tiles(table, tiles, out)


def second_kernel(table, start, tiles, out):
    out[...] = start[...]
    add_tiles(table, tiles, out)


def whole(value):
    return pl.BlockSpec(value.shape, lambda i, *_: (0,) * len(value.shape), pipeline_mode=pl.Buffered(1))


def columns(rows):
    return pl.BlockSpec((rows, SPAN * TILE), lambda i, *_: (0, i))


def first_sum(table, place, weight, near, far, diag, tiles, shape):
    return pl.pallas_call(
        first_kernel,
        grid_spec=pltpu.PrefetchScalarGridSpec(
            num_scalar_prefetch=2,
            grid=(shape[1] // (SPAN * TILE),),
            in_specs=[
                whole(weight),
                columns(near.shape[0]),
                columns(far.shape[0]),
                whole(diag),
                whole(tiles),
            ],
            out_specs=columns(shape[0]),
        ),
        out_shape=jax.ShapeDtypeStruct(shape, jnp.float32),
        name="first_sum",
    )(table, place, weight, near, far, diag, tiles)


def second_sum(table, start, tiles):
    return pl.pallas_call(
        second_kernel,
        grid_spec=pltpu.PrefetchScalarGridSpec(
            num_scalar_prefetch=1,
            grid=(start.shape[1] // (SPAN * TILE),),
            in_specs=[columns(start.shape[0]), whole(tiles)],
            out_specs=columns(start.shape[0]),
        ),
        out_shape=jax.ShapeDtypeStruct(start.shape, jnp.float32),
        name="second_sum",
    )(table, start, tiles)


def per_device(factor_inv, coupling, first_diag, pattern):
    ny, nz, nc, nx = 4, 8, 2, 4
    yi, zi, ci, xi = (lax.axis_index(a) for a in ("y", "z", "c", "x"))
    scen = ("y", "z", "c")
    count = ny * nz * nc
    here = (yi * nz + zi) * nc + ci
    per_range = 32
    f32 = jnp.float32

    def slabs_of(s):
        return jnp.dot(factor_inv[s], coupling[s], preferred_element_type=f32).astype(jnp.bfloat16)

    slab0 = slabs_of(0)
    slab1 = slabs_of(1)
    block0 = gather_ring4(slab0, "x")

    def product(block, slab):
        return jnp.einsum("nr,nc->rc", block, slab, preferred_element_type=f32)

    def spread(block, slab):
        made = jnp.stack([product(block[-j % nx], slab) for j in range(nx)])
        made = (made * SCALE).astype(jnp.float16).reshape(nx, 2, TILE, 2 * TILE)
        made = jnp.stack(
            [lax.dynamic_index_in_dim(made, lax.rem(r - xi + nx, nx), 0, keepdims=False) for r in range(ny)]
        )
        return lax.all_to_all(made, "y", 0, 0, tiled=True)

    near0 = spread(block0, slab0)
    block1 = gather_ring4(after(slab1, block0[2]), "x", near0)

    lead = jnp.where(
        xi == 0, block0[0], jnp.where(xi == 1, block0[1], jnp.where(xi == 2, block0[2], block0[3]))
    )[:, :TILE]
    corner = product(lead, lead)
    unit = jnp.eye(TILE, dtype=f32)
    corner = corner + jnp.where(here == 0, 1.0, 0.0) * (first_diag[0][:, None] * unit)
    top = jnp.concatenate([product(lead, slab0), corner], axis=1).reshape(count, 6, TILE)
    said = jnp.pad(pattern.reshape(1, 1, -1).astype(f32), ((0, 0), (0, 1), (0, TILE - 16)))
    top = jnp.concatenate([top, jnp.broadcast_to(said, (count, 2, TILE))], axis=1)
    top = lax.all_to_all(top, scen, 0, 0, tiled=True)
    names = top[:, 6, :16].astype(jnp.int32).reshape(ny, nz, nc, 2, 8)
    firsts = lax.dynamic_slice_in_dim(names[..., 0, :], xi * 2, 2, 3) - xi * per_range
    firsts = firsts.reshape(-1)
    pick = (jnp.arange(per_range)[:, None] == firsts[None, :]).astype(f32)
    parts = top[:, :6].reshape(count, 2, 3, TILE)
    tiles = parts[:, :, :2].transpose(0, 2, 1, 3).reshape(count * 2, 2 * TILE)
    rows = jnp.dot(pick, tiles, precision=HIGH, preferred_element_type=f32)
    rows = rows.reshape(per_range, 2, TILE).transpose(1, 0, 2).reshape(2, per_range * TILE)
    summed = jnp.sum(parts[:, :, 2], axis=0)
    rows = jnp.concatenate(
        [jnp.where(xi == 0, summed, rows[:, :TILE]), rows[:, TILE:], summed], axis=1
    )
    rows = copies(rows, "z", nz).reshape(2 * nz, -1)
    near = copies(rows, "y", ny).reshape(count, -1)
    far = shifted(near, "c", nc, 1)

    def in_order(value):
        value = value.reshape(nc, ny * nz, 2, -1)
        value = jnp.where(ci == 0, value, value[::-1])
        return value.transpose(1, 0, 2, 3).reshape(TILE, -1)

    def as_lies(value):
        value = value.reshape(ny * nz, nc, 2, -1).transpose(1, 0, 2, 3)
        value = jnp.where(ci == 0, value, value[::-1])
        return value.reshape(TILE, -1)

    edge = per_range * TILE
    own = lax.rem(here, 16) * 2 * TILE
    own = jnp.concatenate(
        [lax.dynamic_slice_in_dim(v, own, 2 * TILE, 1) for v in (near, far)], axis=0
    )
    own = lax.dynamic_index_in_dim(copies(own, "x", nx), yi, 0, keepdims=False)
    factor = jnp.linalg.cholesky(in_order(jnp.concatenate([near[:, edge:], far[:, edge:]], axis=0)))

    bulk0 = gather_ring8(near0, "z")
    bulk1 = gather_ring8(spread(block1, slab1), "z")

    inverse = jax.scipy.linalg.solve_triangular(factor, unit, lower=True)
    solved = jnp.dot(inverse, in_order(own), precision=HIGH, preferred_element_type=f32)
    solved = jnp.concatenate(
        [jnp.where(here == 0, factor.T, solved[:, :TILE]), solved[:, TILE:]], axis=1
    )
    panel = solved.T
    weight = as_lies(jnp.dot(inverse.T, solved, precision=HIGH, preferred_element_type=f32))

    def matches(owner):
        mine = lax.dynamic_slice_in_dim(names, yi * 2, 2, 4)
        return mine // 2 == owner, mine % 2

    to_me, parity = matches(here)
    to_other, _ = matches(here + 1 - 2 * ci)
    to_other = lax.dynamic_index_in_dim(to_other, ci, 2, keepdims=False)
    cols = lax.dynamic_slice_in_dim(names, xi * 2, 2, 4) - xi * per_range
    hit = to_me.astype(jnp.int32)
    fields = jnp.stack(
        [
            jnp.sum(hit, axis=(3, 4)),
            jnp.sum(hit * parity, axis=(3, 4)),
            jnp.sum(jnp.sum(hit, axis=4) * cols[..., 0], axis=3),
            jnp.sum(jnp.sum(hit, axis=4) * cols[..., 1], axis=3),
        ]
    )
    back = lax.rem(zi - jnp.arange(nz) + nz, nz)
    fields = jnp.take(fields, back, axis=2).transpose(0, 3, 2, 1)
    fields = jnp.where(ci == 0, fields, fields[:, ::-1])
    to_me = jnp.take(lax.dynamic_index_in_dim(to_me, ci, 2, keepdims=False), back, axis=1)
    to_other = jnp.take(to_other, back, axis=1)

    def choose(k, match):
        def flag(s, t):
            return match[:, k, s, t][:, None, None]

        first, second = bulk0[k], bulk1[k]
        return jnp.where(
            flag(0, 0),
            first[:, 0],
            jnp.where(flag(0, 1), first[:, 1], jnp.where(flag(1, 0), second[:, 0], second[:, 1])),
        )

    def batch(ks):
        mine = jnp.concatenate([choose(k, to_me) for k in ks], axis=0)
        other = jnp.concatenate([choose(k, to_other) for k in ks], axis=0)
        both = jnp.concatenate([mine, shifted(other, "c", nc, 1)], axis=0)
        table = jnp.concatenate([fields[:, :, k] for k in ks], axis=2)
        return table.reshape(4, -1), both.astype(f32) * (1.0 / SCALE)

    early = [batch((0, 1, 7)), batch((2, 6))]
    first_table = jnp.concatenate([e[0] for e in early], axis=1)
    first_tiles = jnp.concatenate([e[1] for e in early], axis=0)
    last_table, last_tiles = batch((3, 5, 4))
    place = (here * 2 - xi * per_range).astype(jnp.int32)[None]
    start = first_sum(
        first_table, place, weight, near, far, first_diag, first_tiles, (2 * TILE, per_range * TILE)
    )
    return panel, second_sum(last_table, start, last_tiles)


def solution(mesh):
    grid = Mesh(mesh.devices.reshape(4, 8, 2, 4), ("y", "z", "c", "x"))
    scen = ("y", "z", "c")
    in_specs = (P(scen, None, None), P(scen, None, "x"), P(scen, None), P(scen, None))
    out_specs = (P(scen, None), P(scen, "x"))
    return jax.shard_map(
        per_device, mesh=grid, in_specs=in_specs, out_specs=out_specs, check_vma=False
    )
```

```python
import jax
import jax.numpy as jnp
from jax import lax
from jax.experimental import pallas as pl
from jax.experimental.pallas import tpu as pltpu
from jax.sharding import Mesh, PartitionSpec as P

SCALE = 2.0**-7
HIGH = lax.Precision.HIGHEST
TILE = 128
SPAN = 8


def ring(count, shift):
    return [(i, (i + shift) % count) for i in range(count)]


def shifted(value, axis, count, shift):
    return lax.ppermute(value, axis, ring(count, shift))


def exchanged(value, axis):
    return lax.all_to_all(value, axis, 0, 0, tiled=True)


def after(value, *others):
    return lax.optimization_barrier((value,) + others)[0]


def copies(value, axis, count):
    return exchanged(jnp.broadcast_to(value[None], (count,) + value.shape), axis)


def gather_ring4(value, axis, *others):
    half = value.shape[0] // 2
    low = shifted(value, axis, 4, 1)
    high = shifted(value, axis, 4, -1)
    low, high = lax.optimization_barrier((low, high) + others)[:2]
    across = jnp.concatenate(
        [shifted(low[:half], axis, 4, 1), shifted(high[half:], axis, 4, -1)],
        axis=0,
    )
    return [value, low, across, high]


def gather_ring8(value, axis, gates):
    half = value.shape[0] // 2
    got = [value] + [None] * 7
    low = high = value
    for k in range(1, 4):
        low = shifted(low, axis, 8, 1)
        high = shifted(high, axis, 8, -1)
        low, high = lax.optimization_barrier((low, high) + gates.get(k, ()))[:2]
        got[k], got[8 - k] = low, high
    got[4] = jnp.concatenate(
        [shifted(low[:half], axis, 8, 1), shifted(high[half:], axis, 8, -1)],
        axis=0,
    )
    return got


def add_tiles(table, tiles, out):
    first = pl.program_id(0) * SPAN

    def one(source, carry):
        row = pl.multiple_of(table[1, source] * TILE, TILE)
        for t in range(2):
            at = table[2 + t, source] - first

            @pl.when((table[0, source] > 0) & (at >= 0) & (at < SPAN))
            def _():
                col = pl.multiple_of(at * TILE, TILE)
                out[pl.ds(row, TILE), pl.ds(col, TILE)] += tiles[
                    source, :, t * TILE : (t + 1) * TILE
                ]

        return carry

    lax.fori_loop(0, tiles.shape[0], one, 0)


def first_kernel(table, place, weight, near, far, diag, tiles, out):

    def product(q, carry):
        span = pl.ds(pl.multiple_of(q * 2 * TILE, 2 * TILE), 2 * TILE)
        out[:, span] = -lax.dot_general(
            weight[...],
            jnp.concatenate([near[:, span], far[:, span]], axis=0),
            (((0,), (0,)), ((), ())),
            precision=HIGH,
            preferred_element_type=jnp.float32,
        )
        return carry

    lax.fori_loop(0, SPAN // 2, product, 0)
    same = lax.broadcasted_iota(jnp.int32, (TILE, TILE), 0) == lax.broadcasted_iota(
        jnp.int32, (TILE, TILE), 1
    )
    for i in range(2):
        at = place[0] + i - pl.program_id(0) * SPAN

        @pl.when((at >= 0) & (at < SPAN))
        def _():
            col = pl.multiple_of(at * TILE, TILE)
            out[i * TILE : (i + 1) * TILE, pl.ds(col, TILE)] += jnp.where(
                same, diag[i : i + 1, :], 0.0
            )

    add_tiles(table, tiles, out)


def second_kernel(table, start, tiles, out):
    out[...] = start[...]
    add_tiles(table, tiles, out)


def whole(value):
    return pl.BlockSpec(value.shape, lambda i, *_: (0,) * len(value.shape), pipeline_mode=pl.Buffered(1))


def columns(rows):
    return pl.BlockSpec((rows, SPAN * TILE), lambda i, *_: (0, i))


def first_sum(table, place, weight, near, far, diag, tiles, shape):
    return pl.pallas_call(
        first_kernel,
        grid_spec=pltpu.PrefetchScalarGridSpec(
            num_scalar_prefetch=2,
            grid=(shape[1] // (SPAN * TILE),),
            in_specs=[
                whole(weight),
                columns(near.shape[0]),
                columns(far.shape[0]),
                whole(diag),
                whole(tiles),
            ],
            out_specs=columns(shape[0]),
        ),
        out_shape=jax.ShapeDtypeStruct(shape, jnp.float32),
        name="first_sum",
    )(table, place, weight, near, far, diag, tiles)


def second_sum(table, start, tiles):
    return pl.pallas_call(
        second_kernel,
        grid_spec=pltpu.PrefetchScalarGridSpec(
            num_scalar_prefetch=1,
            grid=(start.shape[1] // (SPAN * TILE),),
            in_specs=[columns(start.shape[0]), whole(tiles)],
            out_specs=columns(start.shape[0]),
        ),
        out_shape=jax.ShapeDtypeStruct(start.shape, jnp.float32),
        name="second_sum",
    )(table, start, tiles)


def per_device(factor_inv, coupling, first_diag, pattern):
    ny, nz, nc, nx = 4, 8, 2, 4
    yi, zi, ci, xi = (lax.axis_index(a) for a in ("y", "z", "c", "x"))
    count = ny * nz * nc
    here = (yi * nz + zi) * nc + ci
    per_range = 32
    f32 = jnp.float32

    def slabs_of(s):
        return jnp.dot(factor_inv[s], coupling[s], preferred_element_type=f32).astype(jnp.bfloat16)

    slab0 = slabs_of(0)
    slab1 = slabs_of(1)
    block0 = gather_ring4(slab0, "x", slab1)

    def product(block, slab):
        return jnp.einsum("nr,nc->rc", block, slab, preferred_element_type=f32)

    def spread(block, slab):
        made = jnp.stack([product(block[-j % nx], slab) for j in range(nx)])
        made = (made * SCALE).astype(jnp.float16).reshape(nx, 2, TILE, 2 * TILE)
        made = jnp.stack(
            [lax.dynamic_index_in_dim(made, lax.rem(r - xi + nx, nx), 0, keepdims=False) for r in range(ny)]
        )
        return exchanged(made, "y")

    near0 = spread(block0, slab0)
    block1 = gather_ring4(after(slab1, block0[2]), "x", near0)

    lead = jnp.where(
        xi == 0, block0[0], jnp.where(xi == 1, block0[1], jnp.where(xi == 2, block0[2], block0[3]))
    )[:, :TILE]
    corner = product(lead, lead)
    unit = jnp.eye(TILE, dtype=f32)
    corner = corner + jnp.where(here == 0, 1.0, 0.0) * (first_diag[0][:, None] * unit)
    top = jnp.concatenate([product(lead, slab0), corner], axis=1).reshape(count, 6, TILE)
    said = jnp.pad(pattern.reshape(1, 1, -1).astype(f32), ((0, 0), (0, 1), (0, TILE - 16)))
    top = jnp.concatenate([top, jnp.broadcast_to(said, (count, 2, TILE))], axis=1)
    top = after(top, block1[1], block1[3]).reshape(ny, nz, nc, 8, TILE).transpose(0, 2, 1, 3, 4)
    top = exchanged(top.reshape(ny * nc, nz, 8, TILE), ("y", "c"))
    top = exchanged(top.transpose(1, 0, 2, 3), "z")
    top = top.reshape(count, 8, TILE)
    names = top[:, 6, :16]
    entry = jnp.arange(16, dtype=jnp.int32)[None, :]
    firsts = [
        jnp.sum(jnp.where(entry == xi * 2 + t, names, 0.0), axis=1) - xi * per_range for t in range(2)
    ]
    firsts = jnp.stack(firsts, axis=1).reshape(-1)
    pick = (jnp.arange(per_range, dtype=f32)[:, None] == firsts[None, :]).astype(f32)
    parts = top[:, :6].reshape(count, 2, 3, TILE)
    tiles = parts[:, :, :2].transpose(0, 2, 1, 3).reshape(count * 2, 2 * TILE)
    rows = jnp.dot(pick, tiles, precision=HIGH, preferred_element_type=f32)
    rows = rows.reshape(per_range, 2, TILE).transpose(1, 0, 2).reshape(2, per_range * TILE)
    summed = jnp.sum(parts[:, :, 2], axis=0)
    rows = jnp.concatenate(
        [jnp.where(xi == 0, summed, rows[:, :TILE]), rows[:, TILE:], summed], axis=1
    )
    rows = copies(rows, "z", nz).reshape(2 * nz, -1)
    near = copies(rows, "y", ny).reshape(count, -1)
    far = shifted(near, "c", nc, 1)

    def in_order(value):
        value = value.reshape(nc, ny * nz, 2, -1)
        value = jnp.where(ci == 0, value, value[::-1])
        return value.transpose(1, 0, 2, 3).reshape(TILE, -1)

    def as_lies(value):
        value = value.reshape(ny * nz, nc, 2, -1).transpose(1, 0, 2, 3)
        value = jnp.where(ci == 0, value, value[::-1])
        return value.reshape(TILE, -1)

    edge = per_range * TILE
    own = lax.dynamic_slice_in_dim(near, lax.rem(here - ci, 16) * 2 * TILE, 4 * TILE, 1)
    own = lax.dynamic_index_in_dim(copies(own, "x", nx), yi, 0, keepdims=False)
    own, others = (own[:, : 2 * TILE], own[:, 2 * TILE :])
    own, others = jnp.where(ci == 0, own, others), jnp.where(ci == 0, others, own)
    own = jnp.concatenate([own, shifted(others, "c", nc, 1)], axis=0)
    factor = jnp.linalg.cholesky(in_order(jnp.concatenate([near[:, edge:], far[:, edge:]], axis=0)))

    bulk0 = gather_ring8(near0, "z", {})
    bulk1 = gather_ring8(spread(block1, slab1), "z", {2: (near,), 3: (far,)})

    inverse = jax.scipy.linalg.solve_triangular(after(factor, bulk1[3], bulk1[5]), unit, lower=True)
    solved = jnp.dot(inverse, in_order(own), precision=HIGH, preferred_element_type=f32)
    solved = jnp.concatenate(
        [jnp.where(here == 0, factor.T, solved[:, :TILE]), solved[:, TILE:]], axis=1
    )
    panel = solved.T
    weight = as_lies(jnp.dot(inverse.T, solved, precision=HIGH, preferred_element_type=f32))

    names = names.reshape(nz, ny * nc * 16)
    names = jnp.take(names, lax.rem(zi - jnp.arange(nz) + nz, nz), axis=0).reshape(count, 16)
    in_range = entry % 8 // 2 == yi
    owner = jnp.floor(names * 0.5)
    first_half = entry < 8

    def scattered(owned):
        match = in_range & (owner == owned)
        hits = [
            jnp.sum(jnp.where(match & half, 1.0, 0.0), axis=1, keepdims=True)
            for half in (first_half, ~first_half)
        ]
        return match, hits

    match, hits = scattered(here.astype(f32))
    hit = jnp.where(first_half, hits[0], hits[1])
    fields = [
        (hits[0] + hits[1])[:, 0],
        jnp.sum(jnp.where(match, names - 2.0 * owner, 0.0), axis=1),
        jnp.sum(jnp.where(entry % 8 == xi * 2, hit * (names - xi * per_range), 0.0), axis=1),
        jnp.sum(jnp.where(entry % 8 == xi * 2 + 1, hit * (names - xi * per_range), 0.0), axis=1),
    ]
    fields = jnp.stack(fields).astype(jnp.int32).reshape(4, nz, ny, nc).transpose(0, 3, 1, 2)
    fields = jnp.where(ci == 0, fields, fields[:, ::-1])

    def flags(match):
        match = match.reshape(nz, ny, nc, 2, 8)
        match = lax.dynamic_index_in_dim(match, ci, 2, keepdims=False)
        return lax.dynamic_slice_in_dim(match, yi * 2, 2, 3).transpose(2, 3, 0, 1)

    to_me = flags(match)
    to_other = flags(scattered((here + 1 - 2 * ci).astype(f32))[0])

    def choose(k, match):
        def flag(s, t):
            return match[s, t, k][:, None, None]

        first, second = bulk0[k], bulk1[k]
        return jnp.where(
            flag(0, 0),
            first[:, 0],
            jnp.where(flag(0, 1), first[:, 1], jnp.where(flag(1, 0), second[:, 0], second[:, 1])),
        )

    def batch(ks):
        mine = jnp.concatenate([choose(k, to_me) for k in ks], axis=0)
        other = jnp.concatenate([choose(k, to_other) for k in ks], axis=0)
        both = jnp.concatenate([mine, shifted(other, "c", nc, 1)], axis=0)
        table = jnp.concatenate([fields[:, :, k] for k in ks], axis=2)
        return table.reshape(4, -1), both.astype(f32) * (1.0 / SCALE)

    first_table, first_tiles = batch((0, 1, 7, 2, 6))
    late = [batch((3, 5)), batch((4,))]
    last_table = jnp.concatenate([e[0] for e in late], axis=1)
    last_tiles = jnp.concatenate([e[1] for e in late], axis=0)
    place = (here * 2 - xi * per_range).astype(jnp.int32)[None]
    start = first_sum(
        first_table, place, weight, near, far, first_diag, first_tiles, (2 * TILE, per_range * TILE)
    )
    return panel, second_sum(last_table, start, last_tiles)


def solution(mesh):
    grid = Mesh(mesh.devices.reshape(4, 8, 2, 4), ("y", "z", "c", "x"))
    scen = ("y", "z", "c")
    in_specs = (P(scen, None, None), P(scen, None, "x"), P(scen, None), P(scen, None))
    out_specs = (P(scen, None), P(scen, "x"))

    return jax.shard_map(
        per_device, mesh=grid, in_specs=in_specs, out_specs=out_specs, check_vma=False
    )
```

```python
import jax
import jax.numpy as jnp
from jax import lax
from jax.experimental import pallas as pl
from jax.experimental.pallas import tpu as pltpu
from jax.sharding import Mesh, PartitionSpec as P

SCALE = 2.0**-7
HIGH = lax.Precision.HIGHEST
TILE = 128
SPAN = 8


def ring(count, shift):
    return [(i, (i + shift) % count) for i in range(count)]


def shifted(value, axis, count, shift):
    return lax.ppermute(value, axis, ring(count, shift))


def exchanged(value, axis):
    return lax.all_to_all(value, axis, 0, 0, tiled=True)


def after(value, *others):
    return lax.optimization_barrier((value,) + others)[0]


def copies(value, axis, count):
    return exchanged(jnp.broadcast_to(value[None], (count,) + value.shape), axis)


def gather_ring4(value, axis, *others):
    half = value.shape[0] // 2
    low = shifted(value, axis, 4, 1)
    high = shifted(value, axis, 4, -1)
    low, high = lax.optimization_barrier((low, high) + others)[:2]
    across = jnp.concatenate(
        [shifted(low[:half], axis, 4, 1), shifted(high[half:], axis, 4, -1)],
        axis=0,
    )
    return [value, low, across, high]


def gather_ring8(value, axis, gates):
    half = value.shape[0] // 2
    got = [value] + [None] * 7
    low = high = value
    for k in range(1, 4):
        low = shifted(low, axis, 8, 1)
        high = shifted(high, axis, 8, -1)
        low, high = lax.optimization_barrier((low, high) + gates.get(k, ()))[:2]
        got[k], got[8 - k] = low, high
    got[4] = jnp.concatenate(
        [shifted(low[:half], axis, 8, 1), shifted(high[half:], axis, 8, -1)],
        axis=0,
    )
    return got


def add_tiles(table, tiles, out):
    first = pl.program_id(0) * SPAN

    def one(source, carry):
        row = pl.multiple_of(table[1, source] * TILE, TILE)
        for t in range(2):
            at = table[2 + t, source] - first

            @pl.when((table[0, source] > 0) & (at >= 0) & (at < SPAN))
            def _():
                col = pl.multiple_of(at * TILE, TILE)
                out[pl.ds(row, TILE), pl.ds(col, TILE)] += tiles[
                    source, :, t * TILE : (t + 1) * TILE
                ]

        return carry

    lax.fori_loop(0, tiles.shape[0], one, 0)


def first_kernel(table, place, weight, near, far, diag, tiles, out):

    def product(q, carry):
        span = pl.ds(pl.multiple_of(q * 2 * TILE, 2 * TILE), 2 * TILE)
        out[:, span] = -lax.dot_general(
            weight[...],
            jnp.concatenate([near[:, span], far[:, span]], axis=0),
            (((0,), (0,)), ((), ())),
            precision=HIGH,
            preferred_element_type=jnp.float32,
        )
        return carry

    lax.fori_loop(0, SPAN // 2, product, 0)
    same = lax.broadcasted_iota(jnp.int32, (TILE, TILE), 0) == lax.broadcasted_iota(
        jnp.int32, (TILE, TILE), 1
    )
    for i in range(2):
        at = place[0] + i - pl.program_id(0) * SPAN

        @pl.when((at >= 0) & (at < SPAN))
        def _():
            col = pl.multiple_of(at * TILE, TILE)
            out[i * TILE : (i + 1) * TILE, pl.ds(col, TILE)] += jnp.where(
                same, diag[i : i + 1, :], 0.0
            )

    add_tiles(table, tiles, out)


def second_kernel(table, start, tiles, out):
    out[...] = start[...]
    add_tiles(table, tiles, out)


def whole(value):
    return pl.BlockSpec(value.shape, lambda i, *_: (0,) * len(value.shape), pipeline_mode=pl.Buffered(1))


def columns(rows):
    return pl.BlockSpec((rows, SPAN * TILE), lambda i, *_: (0, i))


def first_sum(table, place, weight, near, far, diag, tiles, shape):
    return pl.pallas_call(
        first_kernel,
        grid_spec=pltpu.PrefetchScalarGridSpec(
            num_scalar_prefetch=2,
            grid=(shape[1] // (SPAN * TILE),),
            in_specs=[
                whole(weight),
                columns(near.shape[0]),
                columns(far.shape[0]),
                whole(diag),
                whole(tiles),
            ],
            out_specs=columns(shape[0]),
        ),
        out_shape=jax.ShapeDtypeStruct(shape, jnp.float32),
        name="first_sum",
    )(table, place, weight, near, far, diag, tiles)


def second_sum(table, start, tiles):
    return pl.pallas_call(
        second_kernel,
        grid_spec=pltpu.PrefetchScalarGridSpec(
            num_scalar_prefetch=1,
            grid=(start.shape[1] // (SPAN * TILE),),
            in_specs=[columns(start.shape[0]), whole(tiles)],
            out_specs=columns(start.shape[0]),
        ),
        out_shape=jax.ShapeDtypeStruct(start.shape, jnp.float32),
        name="second_sum",
    )(table, start, tiles)


def per_device(factor_inv, coupling, first_diag, pattern):
    ny, nz, nc, nx = 4, 8, 2, 4
    yi, zi, ci, xi = (lax.axis_index(a) for a in ("y", "z", "c", "x"))
    count = ny * nz * nc
    here = (yi * nz + zi) * nc + ci
    per_range = 32
    f32 = jnp.float32

    def slabs_of(s):
        return jnp.dot(factor_inv[s], coupling[s], preferred_element_type=f32).astype(jnp.bfloat16)

    slab0 = slabs_of(0)
    slab1 = slabs_of(1)
    block0 = gather_ring4(slab0, "x", slab1)

    def product(block, slab):
        return jnp.einsum("nr,nc->rc", block, slab, preferred_element_type=f32)

    block1 = gather_ring4(after(slab1, block0[2]), "x")

    lead = jnp.where(
        xi == 0, block0[0], jnp.where(xi == 1, block0[1], jnp.where(xi == 2, block0[2], block0[3]))
    )[:, :TILE]
    corner = product(lead, lead)
    unit = jnp.eye(TILE, dtype=f32)
    corner = corner + jnp.where(here == 0, 1.0, 0.0) * (first_diag[0][:, None] * unit)
    top = jnp.concatenate([product(lead, slab0), corner], axis=1).reshape(count, 6, TILE)
    said = jnp.pad(pattern.reshape(1, 1, -1).astype(f32), ((0, 0), (0, 1), (0, TILE - 16)))
    top = jnp.concatenate([top, jnp.broadcast_to(said, (count, 2, TILE))], axis=1)
    top = top.reshape(ny, nz, nc, 8, TILE).transpose(0, 2, 1, 3, 4)
    top = exchanged(top.reshape(ny * nc, nz, 8, TILE), ("y", "c"))
    top = exchanged(top.transpose(1, 0, 2, 3), "z")
    top = top.reshape(count, 8, TILE)
    names = top[:, 6, :16]
    entry = jnp.arange(16, dtype=jnp.int32)[None, :]
    firsts = [
        jnp.sum(jnp.where(entry == xi * 2 + t, names, 0.0), axis=1) - xi * per_range for t in range(2)
    ]
    firsts = jnp.stack(firsts, axis=1).reshape(-1)
    pick = (jnp.arange(per_range, dtype=f32)[:, None] == firsts[None, :]).astype(f32)
    parts = top[:, :6].reshape(count, 2, 3, TILE)
    tiles = parts[:, :, :2].transpose(0, 2, 1, 3).reshape(count * 2, 2 * TILE)
    rows = jnp.dot(pick, tiles, precision=HIGH, preferred_element_type=f32)
    rows = rows.reshape(per_range, 2, TILE).transpose(1, 0, 2).reshape(2, per_range * TILE)
    summed = jnp.sum(parts[:, :, 2], axis=0)
    rows = jnp.concatenate(
        [jnp.where(xi == 0, summed, rows[:, :TILE]), rows[:, TILE:], summed], axis=1
    )
    rows = copies(rows, "z", nz).reshape(2 * nz, -1)

    made = jnp.stack(
        [
            jnp.stack([product(b[-j % nx], slab) for b, slab in ((block0, slab0), (block1, slab1))])
            for j in range(nx)
        ]
    )
    made = (made * SCALE).astype(jnp.float16).reshape(nx, 2, 2, TILE, 2 * TILE)
    made = jnp.stack(
        [
            lax.dynamic_index_in_dim(made, lax.rem(r - xi + nx, nx), 0, keepdims=False)
            for r in range(ny)
        ]
    )
    picked = exchanged(made, "y")

    near = copies(after(rows, picked), "y", ny).reshape(count, -1)
    far = shifted(near, "c", nc, 1)

    def in_order(value):
        value = value.reshape(nc, ny * nz, 2, -1)
        value = jnp.where(ci == 0, value, value[::-1])
        return value.transpose(1, 0, 2, 3).reshape(TILE, -1)

    def as_lies(value):
        value = value.reshape(ny * nz, nc, 2, -1).transpose(1, 0, 2, 3)
        value = jnp.where(ci == 0, value, value[::-1])
        return value.reshape(TILE, -1)

    edge = per_range * TILE
    own = lax.dynamic_slice_in_dim(near, lax.rem(here - ci, 16) * 2 * TILE, 4 * TILE, 1)
    own = lax.dynamic_index_in_dim(copies(own, "x", nx), yi, 0, keepdims=False)
    own, others = (own[:, : 2 * TILE], own[:, 2 * TILE :])
    own, others = jnp.where(ci == 0, own, others), jnp.where(ci == 0, others, own)
    own = jnp.concatenate([own, shifted(others, "c", nc, 1)], axis=0)
    bulk = gather_ring8(picked, "z", {2: (far,)})
    corner = in_order(jnp.concatenate([near[:, edge:], far[:, edge:]], axis=0))
    factor = jnp.linalg.cholesky(after(corner, bulk[1], bulk[7]))

    inverse = jax.scipy.linalg.solve_triangular(after(factor, bulk[2], bulk[6]), unit, lower=True)
    solved = jnp.dot(inverse, in_order(own), precision=HIGH, preferred_element_type=f32)
    solved = jnp.concatenate(
        [jnp.where(here == 0, factor.T, solved[:, :TILE]), solved[:, TILE:]], axis=1
    )
    panel = solved.T
    weight = as_lies(jnp.dot(inverse.T, solved, precision=HIGH, preferred_element_type=f32))

    names = names.reshape(nz, ny * nc * 16)
    names = jnp.take(names, lax.rem(zi - jnp.arange(nz) + nz, nz), axis=0).reshape(count, 16)
    in_range = entry % 8 // 2 == yi
    owner = jnp.floor(names * 0.5)
    first_half = entry < 8

    def scattered(owned):
        match = in_range & (owner == owned)
        hits = [
            jnp.sum(jnp.where(match & half, 1.0, 0.0), axis=1, keepdims=True)
            for half in (first_half, ~first_half)
        ]
        return match, hits

    match, hits = scattered(here.astype(f32))
    hit = jnp.where(first_half, hits[0], hits[1])
    fields = [
        (hits[0] + hits[1])[:, 0],
        jnp.sum(jnp.where(match, names - 2.0 * owner, 0.0), axis=1),
        jnp.sum(jnp.where(entry % 8 == xi * 2, hit * (names - xi * per_range), 0.0), axis=1),
        jnp.sum(jnp.where(entry % 8 == xi * 2 + 1, hit * (names - xi * per_range), 0.0), axis=1),
    ]
    fields = jnp.stack(fields).astype(jnp.int32).reshape(4, nz, ny, nc).transpose(0, 3, 1, 2)
    fields = jnp.where(ci == 0, fields, fields[:, ::-1])

    def flags(match):
        match = match.reshape(nz, ny, nc, 2, 8)
        match = lax.dynamic_index_in_dim(match, ci, 2, keepdims=False)
        return lax.dynamic_slice_in_dim(match, yi * 2, 2, 3).transpose(2, 3, 0, 1)

    to_me = flags(match)
    to_other = flags(scattered((here + 1 - 2 * ci).astype(f32))[0])

    def choose(k, match):
        def flag(s, t):
            return match[s, t, k][:, None, None]

        got = bulk[k]
        second = jnp.where(flag(1, 0), got[:, 1, 0], got[:, 1, 1])
        return jnp.where(flag(0, 0), got[:, 0, 0], jnp.where(flag(0, 1), got[:, 0, 1], second))

    def batch(ks):
        mine = jnp.concatenate([choose(k, to_me) for k in ks], axis=0)
        other = jnp.concatenate([choose(k, to_other) for k in ks], axis=0)
        both = jnp.concatenate([mine, shifted(other, "c", nc, 1)], axis=0)
        table = jnp.concatenate([fields[:, :, k] for k in ks], axis=2)
        return table.reshape(4, -1), both.astype(f32) * (1.0 / SCALE)

    first_table, first_tiles = batch((0, 1, 7, 2, 6))
    late = [batch((3, 5)), batch((4,))]
    last_table = jnp.concatenate([e[0] for e in late], axis=1)
    last_tiles = jnp.concatenate([e[1] for e in late], axis=0)
    place = (here * 2 - xi * per_range).astype(jnp.int32)[None]
    weight = after(weight, bulk[3], bulk[5])
    shape = (2 * TILE, per_range * TILE)
    start = first_sum(first_table, place, weight, near, far, first_diag, first_tiles, shape)
    return panel, second_sum(last_table, start, last_tiles)


def solution(mesh):
    grid = Mesh(mesh.devices.reshape(4, 8, 2, 4), ("y", "z", "c", "x"))
    scen = ("y", "z", "c")
    in_specs = (P(scen, None, None), P(scen, None, "x"), P(scen, None), P(scen, None))
    out_specs = (P(scen, None), P(scen, "x"))

    return jax.shard_map(
        per_device, mesh=grid, in_specs=in_specs, out_specs=out_specs, check_vma=False
    )
```

```python
import jax
import jax.numpy as jnp
from jax import lax
from jax.experimental import pallas as pl
from jax.experimental.pallas import tpu as pltpu
from jax.sharding import Mesh, PartitionSpec as P

SCALE = 2.0**-7
HIGH = lax.Precision.HIGHEST
TILE = 128
SPAN = 8


def ring(count, shift):
    return [(i, (i + shift) % count) for i in range(count)]


def shifted(value, axis, count, shift):
    return lax.ppermute(value, axis, ring(count, shift))


def exchanged(value, axis):
    return lax.all_to_all(value, axis, 0, 0, tiled=True)


def after(value, *others):
    return lax.optimization_barrier((value,) + others)[0]


def copies(value, axis, count):
    return exchanged(jnp.broadcast_to(value[None], (count,) + value.shape), axis)


def gather_ring4(value, axis, *others):
    half = value.shape[0] // 2
    low = shifted(value, axis, 4, 1)
    high = shifted(value, axis, 4, -1)
    low, high = lax.optimization_barrier((low, high) + others)[:2]
    across = jnp.concatenate(
        [shifted(low[:half], axis, 4, 1), shifted(high[half:], axis, 4, -1)],
        axis=0,
    )
    return [value, low, across, high]


def gather_ring8(value, axis, gates):
    half = value.shape[0] // 2
    got = [value] + [None] * 7
    low = high = value
    for k in range(1, 4):
        low = shifted(low, axis, 8, 1)
        high = shifted(high, axis, 8, -1)
        low, high = lax.optimization_barrier((low, high) + gates.get(k, ()))[:2]
        got[k], got[8 - k] = low, high
    got[4] = jnp.concatenate(
        [shifted(low[:half], axis, 8, 1), shifted(high[half:], axis, 8, -1)],
        axis=0,
    )
    return got


def add_tiles(table, tiles, out):
    first = pl.program_id(0) * SPAN

    def one(source, carry):
        row = pl.multiple_of(table[1, source] * TILE, TILE)
        for t in range(2):
            at = table[2 + t, source] - first

            @pl.when((table[0, source] > 0) & (at >= 0) & (at < SPAN))
            def _():
                col = pl.multiple_of(at * TILE, TILE)
                out[pl.ds(row, TILE), pl.ds(col, TILE)] += tiles[
                    source, :, t * TILE : (t + 1) * TILE
                ]

        return carry

    lax.fori_loop(0, tiles.shape[0], one, 0)


def first_kernel(table, place, weight, near, far, diag, tiles, out):

    def product(q, carry):
        span = pl.ds(pl.multiple_of(q * 2 * TILE, 2 * TILE), 2 * TILE)
        out[:, span] = -lax.dot_general(
            weight[...],
            jnp.concatenate([near[:, span], far[:, span]], axis=0),
            (((0,), (0,)), ((), ())),
            precision=HIGH,
            preferred_element_type=jnp.float32,
        )
        return carry

    lax.fori_loop(0, SPAN // 2, product, 0)
    same = lax.broadcasted_iota(jnp.int32, (TILE, TILE), 0) == lax.broadcasted_iota(
        jnp.int32, (TILE, TILE), 1
    )
    for i in range(2):
        at = place[0] + i - pl.program_id(0) * SPAN

        @pl.when((at >= 0) & (at < SPAN))
        def _():
            col = pl.multiple_of(at * TILE, TILE)
            out[i * TILE : (i + 1) * TILE, pl.ds(col, TILE)] += jnp.where(
                same, diag[i : i + 1, :], 0.0
            )

    add_tiles(table, tiles, out)


def second_kernel(table, start, tiles, out):
    out[...] = start[...]
    add_tiles(table, tiles, out)


def factor_kernel(matrix, upper, inverse, work):
    size = matrix.shape[0]
    work[...] = matrix[...]
    down = lax.broadcasted_iota(jnp.int32, (size, size), 0)
    along = lax.broadcasted_iota(jnp.int32, (size, size), 1)
    inverse[...] = jnp.where(down == along, 1.0, 0.0)
    place = lax.broadcasted_iota(jnp.int32, (1, size), 1)
    depth = lax.broadcasted_iota(jnp.int32, (size, 1), 0)

    def step(j, carry):
        row = work[pl.ds(j, 1), :]
        pivot = jnp.sum(jnp.where(place == j, row, 0.0), axis=1, keepdims=True)
        scale = 1.0 / jnp.sqrt(pivot)
        row = jnp.where(place >= j, row * scale, 0.0)
        column = jnp.sum(jnp.where(along == j, work[...], 0.0), axis=1, keepdims=True)
        column = jnp.where(depth > j, column * scale, 0.0)
        solved = inverse[pl.ds(j, 1), :] * scale
        work[...] -= column * row
        inverse[...] -= column * solved
        inverse[pl.ds(j, 1), :] = solved
        upper[pl.ds(j, 1), :] = row
        return carry

    lax.fori_loop(0, size, step, 0)


def factored(matrix):
    shape = jax.ShapeDtypeStruct(matrix.shape, jnp.float32)
    return pl.pallas_call(
        factor_kernel,
        out_shape=(shape, shape),
        scratch_shapes=[pltpu.VMEM(matrix.shape, jnp.float32)],
        name="factored",
    )(matrix)


def whole(value):
    return pl.BlockSpec(value.shape, lambda i, *_: (0,) * len(value.shape), pipeline_mode=pl.Buffered(1))


def columns(rows):
    return pl.BlockSpec((rows, SPAN * TILE), lambda i, *_: (0, i))


def first_sum(table, place, weight, near, far, diag, tiles, shape):
    return pl.pallas_call(
        first_kernel,
        grid_spec=pltpu.PrefetchScalarGridSpec(
            num_scalar_prefetch=2,
            grid=(shape[1] // (SPAN * TILE),),
            in_specs=[
                whole(weight),
                columns(near.shape[0]),
                columns(far.shape[0]),
                whole(diag),
                whole(tiles),
            ],
            out_specs=columns(shape[0]),
        ),
        out_shape=jax.ShapeDtypeStruct(shape, jnp.float32),
        name="first_sum",
    )(table, place, weight, near, far, diag, tiles)


def second_sum(table, start, tiles):
    return pl.pallas_call(
        second_kernel,
        grid_spec=pltpu.PrefetchScalarGridSpec(
            num_scalar_prefetch=1,
            grid=(start.shape[1] // (SPAN * TILE),),
            in_specs=[columns(start.shape[0]), whole(tiles)],
            out_specs=columns(start.shape[0]),
        ),
        out_shape=jax.ShapeDtypeStruct(start.shape, jnp.float32),
        name="second_sum",
    )(table, start, tiles)


def per_device(factor_inv, coupling, first_diag, pattern):
    ny, nz, nc, nx = 4, 8, 2, 4
    yi, zi, ci, xi = (lax.axis_index(a) for a in ("y", "z", "c", "x"))
    count = ny * nz * nc
    here = (yi * nz + zi) * nc + ci
    per_range = 32
    f32 = jnp.float32

    def slabs_of(s):
        return jnp.dot(factor_inv[s], coupling[s], preferred_element_type=f32).astype(jnp.bfloat16)

    slab0 = slabs_of(0)
    slab1 = slabs_of(1)
    block0 = gather_ring4(slab0, "x", slab1)

    def product(block, slab):
        return jnp.einsum("nr,nc->rc", block, slab, preferred_element_type=f32)

    block1 = gather_ring4(after(slab1, block0[2]), "x")

    lead = jnp.where(
        xi == 0, block0[0], jnp.where(xi == 1, block0[1], jnp.where(xi == 2, block0[2], block0[3]))
    )[:, :TILE]
    corner = product(lead, lead)
    unit = jnp.eye(TILE, dtype=f32)
    corner = corner + jnp.where(here == 0, 1.0, 0.0) * (first_diag[0][:, None] * unit)
    top = jnp.concatenate([product(lead, slab0), corner], axis=1).reshape(count, 6, TILE)
    said = jnp.pad(pattern.reshape(1, 1, -1).astype(f32), ((0, 0), (0, 1), (0, TILE - 16)))
    top = jnp.concatenate([top, jnp.broadcast_to(said, (count, 2, TILE))], axis=1)
    top = top.reshape(ny, nz, nc, 8, TILE).transpose(0, 2, 1, 3, 4)
    top = exchanged(top.reshape(ny * nc, nz, 8, TILE), ("y", "c"))
    top = exchanged(top.transpose(1, 0, 2, 3), "z")
    top = top.reshape(count, 8, TILE)
    names = top[:, 6, :16]
    entry = jnp.arange(16, dtype=jnp.int32)[None, :]
    firsts = [
        jnp.sum(jnp.where(entry == xi * 2 + t, names, 0.0), axis=1) - xi * per_range for t in range(2)
    ]
    firsts = jnp.stack(firsts, axis=1).reshape(-1)
    pick = (jnp.arange(per_range, dtype=f32)[:, None] == firsts[None, :]).astype(f32)
    parts = top[:, :6].reshape(count, 2, 3, TILE)
    tiles = parts[:, :, :2].transpose(0, 2, 1, 3).reshape(count * 2, 2 * TILE)
    rows = jnp.dot(pick, tiles, precision=HIGH, preferred_element_type=f32)
    rows = rows.reshape(per_range, 2, TILE).transpose(1, 0, 2).reshape(2, per_range * TILE)
    summed = jnp.sum(parts[:, :, 2], axis=0)
    rows = jnp.concatenate(
        [jnp.where(xi == 0, summed, rows[:, :TILE]), rows[:, TILE:], summed], axis=1
    )
    rows = copies(rows, "z", nz).reshape(2 * nz, -1)

    made = jnp.stack(
        [
            jnp.stack([product(b[-j % nx], slab) for b, slab in ((block0, slab0), (block1, slab1))])
            for j in range(nx)
        ]
    )
    made = (made * SCALE).astype(jnp.float16).reshape(nx, 2, 2, TILE, 2 * TILE)
    made = jnp.stack(
        [
            lax.dynamic_index_in_dim(made, lax.rem(r - xi + nx, nx), 0, keepdims=False)
            for r in range(ny)
        ]
    )
    picked = exchanged(made, "y")

    near = copies(after(rows, picked), "y", ny).reshape(count, -1)
    far = shifted(near, "c", nc, 1)

    def in_order(value):
        value = value.reshape(nc, ny * nz, 2, -1)
        value = jnp.where(ci == 0, value, value[::-1])
        return value.transpose(1, 0, 2, 3).reshape(TILE, -1)

    def as_lies(value):
        value = value.reshape(ny * nz, nc, 2, -1).transpose(1, 0, 2, 3)
        value = jnp.where(ci == 0, value, value[::-1])
        return value.reshape(TILE, -1)

    edge = per_range * TILE
    own = lax.dynamic_slice_in_dim(near, lax.rem(here - ci, 16) * 2 * TILE, 4 * TILE, 1)
    own = lax.dynamic_index_in_dim(copies(own, "x", nx), yi, 0, keepdims=False)
    own, others = (own[:, : 2 * TILE], own[:, 2 * TILE :])
    own, others = jnp.where(ci == 0, own, others), jnp.where(ci == 0, others, own)
    own = jnp.concatenate([own, shifted(others, "c", nc, 1)], axis=0)
    bulk = gather_ring8(picked, "z", {2: (far,)})
    corner = in_order(jnp.concatenate([near[:, edge:], far[:, edge:]], axis=0))
    upper, inverse = factored(after(corner, bulk[1], bulk[7]))
    solved = jnp.dot(inverse, in_order(own), precision=HIGH, preferred_element_type=f32)
    solved = jnp.concatenate(
        [jnp.where(here == 0, upper, solved[:, :TILE]), solved[:, TILE:]], axis=1
    )
    panel = solved.T
    weight = as_lies(jnp.dot(inverse.T, solved, precision=HIGH, preferred_element_type=f32))

    names = names.reshape(nz, ny * nc * 16)
    names = jnp.take(names, lax.rem(zi - jnp.arange(nz) + nz, nz), axis=0).reshape(count, 16)
    in_range = entry % 8 // 2 == yi
    owner = jnp.floor(names * 0.5)
    first_half = entry < 8

    def scattered(owned):
        match = in_range & (owner == owned)
        hits = [
            jnp.sum(jnp.where(match & half, 1.0, 0.0), axis=1, keepdims=True)
            for half in (first_half, ~first_half)
        ]
        return match, hits

    match, hits = scattered(here.astype(f32))
    hit = jnp.where(first_half, hits[0], hits[1])
    fields = [
        (hits[0] + hits[1])[:, 0],
        jnp.sum(jnp.where(match, names - 2.0 * owner, 0.0), axis=1),
        jnp.sum(jnp.where(entry % 8 == xi * 2, hit * (names - xi * per_range), 0.0), axis=1),
        jnp.sum(jnp.where(entry % 8 == xi * 2 + 1, hit * (names - xi * per_range), 0.0), axis=1),
    ]
    fields = jnp.stack(fields).astype(jnp.int32).reshape(4, nz, ny, nc).transpose(0, 3, 1, 2)
    fields = jnp.where(ci == 0, fields, fields[:, ::-1])

    def flags(match):
        match = match.reshape(nz, ny, nc, 2, 8)
        match = lax.dynamic_index_in_dim(match, ci, 2, keepdims=False)
        return lax.dynamic_slice_in_dim(match, yi * 2, 2, 3).transpose(2, 3, 0, 1)

    to_me = flags(match)
    to_other = flags(scattered((here + 1 - 2 * ci).astype(f32))[0])

    def choose(k, match):
        def flag(s, t):
            return match[s, t, k][:, None, None]

        got = bulk[k]
        second = jnp.where(flag(1, 0), got[:, 1, 0], got[:, 1, 1])
        return jnp.where(flag(0, 0), got[:, 0, 0], jnp.where(flag(0, 1), got[:, 0, 1], second))

    def batch(ks):
        mine = jnp.concatenate([choose(k, to_me) for k in ks], axis=0)
        other = jnp.concatenate([choose(k, to_other) for k in ks], axis=0)
        both = jnp.concatenate([mine, shifted(other, "c", nc, 1)], axis=0)
        table = jnp.concatenate([fields[:, :, k] for k in ks], axis=2)
        return table.reshape(4, -1), both.astype(f32) * (1.0 / SCALE)

    first_table, first_tiles = batch((0, 1, 7, 2, 6))
    place = (here * 2 - xi * per_range).astype(jnp.int32)[None]
    weight = after(weight, bulk[3], bulk[5])
    shape = (2 * TILE, per_range * TILE)
    start = first_sum(first_table, place, weight, near, far, first_diag, first_tiles, shape)
    late = [batch((3, 5))]
    bulk[4] = after(bulk[4], start)
    late.append(batch((4,)))
    last_table = jnp.concatenate([e[0] for e in late], axis=1)
    last_tiles = jnp.concatenate([e[1] for e in late], axis=0)
    return panel, second_sum(last_table, start, last_tiles)


def solution(mesh):
    grid = Mesh(mesh.devices.reshape(4, 8, 2, 4), ("y", "z", "c", "x"))
    scen = ("y", "z", "c")
    in_specs = (P(scen, None, None), P(scen, None, "x"), P(scen, None), P(scen, None))
    out_specs = (P(scen, None), P(scen, "x"))

    return jax.shard_map(
        per_device, mesh=grid, in_specs=in_specs, out_specs=out_specs, check_vma=False
    )
```

```python
import jax
import jax.numpy as jnp
from jax import lax
from jax.experimental import pallas as pl
from jax.experimental.pallas import tpu as pltpu
from jax.sharding import Mesh, PartitionSpec as P

SCALE = 2.0**-7
HIGH = lax.Precision.HIGHEST
TILE = 128
SPAN = 8


def ring(count, shift):
    return [(i, (i + shift) % count) for i in range(count)]


def shifted(value, axis, count, shift):
    return lax.ppermute(value, axis, ring(count, shift))


def exchanged(value, axis):
    return lax.all_to_all(value, axis, 0, 0, tiled=True)


def after(value, *others):
    return lax.optimization_barrier((value,) + others)[0]


def copies(value, axis, count):
    return exchanged(jnp.broadcast_to(value[None], (count,) + value.shape), axis)


def gather_ring4(value, axis, *others):
    half = value.shape[0] // 2
    low = shifted(value, axis, 4, 1)
    high = shifted(value, axis, 4, -1)
    low, high = lax.optimization_barrier((low, high) + others)[:2]
    across = jnp.concatenate(
        [shifted(low[:half], axis, 4, 1), shifted(high[half:], axis, 4, -1)],
        axis=0,
    )
    return [value, low, across, high]


def add_tiles(table, tiles, out):
    first = pl.program_id(0) * SPAN

    def one(source, carry):
        row = pl.multiple_of(table[1, source] * TILE, TILE)
        for t in range(2):
            at = table[2 + t, source] - first

            @pl.when((table[0, source] > 0) & (at >= 0) & (at < SPAN))
            def _():
                col = pl.multiple_of(at * TILE, TILE)
                out[pl.ds(row, TILE), pl.ds(col, TILE)] += tiles[
                    source, :, t * TILE : (t + 1) * TILE
                ]

        return carry

    lax.fori_loop(0, tiles.shape[0], one, 0)


def first_kernel(table, place, weight, near, far, diag, tiles, out):

    def product(q, carry):
        span = pl.ds(pl.multiple_of(q * 4 * TILE, 4 * TILE), 4 * TILE)
        out[:, span] = -lax.dot_general(
            weight[...],
            jnp.concatenate([near[:, span], far[:, span]], axis=0),
            (((1,), (0,)), ((), ())),
            precision=HIGH,
            preferred_element_type=jnp.float32,
        )
        return carry

    lax.fori_loop(0, SPAN // 4, product, 0)
    same = lax.broadcasted_iota(jnp.int32, (TILE, TILE), 0) == lax.broadcasted_iota(
        jnp.int32, (TILE, TILE), 1
    )
    for i in range(2):
        at = place[0] + i - pl.program_id(0) * SPAN

        @pl.when((at >= 0) & (at < SPAN))
        def _():
            col = pl.multiple_of(at * TILE, TILE)
            out[i * TILE : (i + 1) * TILE, pl.ds(col, TILE)] += jnp.where(
                same, diag[i : i + 1, :], 0.0
            )

    add_tiles(table, tiles, out)


def second_kernel(table, start, tiles, out):
    out[...] = start[...]
    add_tiles(table, tiles, out)


def factor_kernel(matrix, upper, inverse, work):
    size = matrix.shape[0]
    work[...] = matrix[...]
    down = lax.broadcasted_iota(jnp.int32, (size, size), 0)
    along = lax.broadcasted_iota(jnp.int32, (size, size), 1)
    inverse[...] = jnp.where(down == along, 1.0, 0.0)
    place = lax.broadcasted_iota(jnp.int32, (1, size), 1)
    depth = lax.broadcasted_iota(jnp.int32, (size, 1), 0)

    def step(j, carry):
        row = work[pl.ds(j, 1), :]
        pivot = jnp.sum(jnp.where(place == j, row, 0.0), axis=1, keepdims=True)
        scale = 1.0 / jnp.sqrt(pivot)
        row = jnp.where(place >= j, row * scale, 0.0)
        column = jnp.sum(jnp.where(along == j, work[...], 0.0), axis=1, keepdims=True)
        column = jnp.where(depth > j, column * scale, 0.0)
        solved = inverse[pl.ds(j, 1), :] * scale
        work[...] -= column * row
        inverse[...] -= column * solved
        inverse[pl.ds(j, 1), :] = solved
        upper[pl.ds(j, 1), :] = row
        return carry

    lax.fori_loop(0, size, step, 0)


def factored(matrix):
    shape = jax.ShapeDtypeStruct(matrix.shape, jnp.float32)
    return pl.pallas_call(
        factor_kernel,
        out_shape=(shape, shape),
        scratch_shapes=[pltpu.VMEM(matrix.shape, jnp.float32)],
        name="factored",
    )(matrix)


def whole(value):
    return pl.BlockSpec(value.shape, lambda i, *_: (0,) * len(value.shape), pipeline_mode=pl.Buffered(1))


def columns(rows):
    return pl.BlockSpec((rows, SPAN * TILE), lambda i, *_: (0, i))


def first_sum(table, place, weight, near, far, diag, tiles, shape):
    return pl.pallas_call(
        first_kernel,
        grid_spec=pltpu.PrefetchScalarGridSpec(
            num_scalar_prefetch=2,
            grid=(shape[1] // (SPAN * TILE),),
            in_specs=[
                whole(weight),
                columns(near.shape[0]),
                columns(far.shape[0]),
                whole(diag),
                whole(tiles),
            ],
            out_specs=columns(shape[0]),
        ),
        out_shape=jax.ShapeDtypeStruct(shape, jnp.float32),
        name="first_sum",
    )(table, place, weight, near, far, diag, tiles)


def second_sum(table, start, tiles):
    return pl.pallas_call(
        second_kernel,
        grid_spec=pltpu.PrefetchScalarGridSpec(
            num_scalar_prefetch=1,
            grid=(start.shape[1] // (SPAN * TILE),),
            in_specs=[columns(start.shape[0]), whole(tiles)],
            out_specs=columns(start.shape[0]),
        ),
        out_shape=jax.ShapeDtypeStruct(start.shape, jnp.float32),
        name="second_sum",
    )(table, start, tiles)


def per_device(factor_inv, coupling, first_diag, pattern):
    ny, nz, nc, nx = 4, 8, 2, 4
    yi, zi, ci, xi = (lax.axis_index(a) for a in ("y", "z", "c", "x"))
    count = ny * nz * nc
    here = (yi * nz + zi) * nc + ci
    per_range = 32
    f32 = jnp.float32

    def slabs_of(s):
        return jnp.dot(factor_inv[s], coupling[s], preferred_element_type=f32).astype(jnp.bfloat16)

    slab0 = slabs_of(0)
    slab1 = slabs_of(1)
    block0 = gather_ring4(slab0, "x", slab1)

    def product(block, slab):
        return jnp.einsum("nr,nc->rc", block, slab, preferred_element_type=f32)

    block1 = gather_ring4(after(slab1, block0[2]), "x")

    lead = jnp.where(
        xi == 0, block0[0], jnp.where(xi == 1, block0[1], jnp.where(xi == 2, block0[2], block0[3]))
    )[:, :TILE]
    corner = product(lead, lead)
    unit = jnp.eye(TILE, dtype=f32)
    corner = corner + jnp.where(here == 0, 1.0, 0.0) * (first_diag[0][:, None] * unit)
    top = jnp.concatenate([product(lead, slab0), corner], axis=1).reshape(count, 6, TILE)
    said = jnp.pad(pattern.reshape(1, 1, -1).astype(f32), ((0, 0), (0, 1), (0, TILE - 16)))
    top = jnp.concatenate([top, jnp.broadcast_to(said, (count, 2, TILE))], axis=1)
    top = top.reshape(ny, nz, nc, 8, TILE).transpose(0, 2, 1, 3, 4)
    top = exchanged(top.reshape(ny * nc, nz, 8, TILE), ("y", "c"))
    top = exchanged(top.transpose(1, 0, 2, 3), "z")
    top = top.reshape(count, 8, TILE)
    names = top[:, 6, :16]
    entry = jnp.arange(16, dtype=jnp.int32)[None, :]
    firsts = [
        jnp.sum(jnp.where(entry == xi * 2 + t, names, 0.0), axis=1) - xi * per_range for t in range(2)
    ]
    firsts = jnp.stack(firsts, axis=1).reshape(-1)
    pick = (jnp.arange(per_range, dtype=f32)[:, None] == firsts[None, :]).astype(f32)
    parts = top[:, :6].reshape(count, 2, 3, TILE)
    tiles = parts[:, :, :2].transpose(0, 2, 1, 3).reshape(count * 2, 2 * TILE)
    rows = jnp.dot(pick, tiles, precision=HIGH, preferred_element_type=f32)
    rows = rows.reshape(per_range, 2, TILE).transpose(1, 0, 2).reshape(2, per_range * TILE)
    summed = jnp.sum(parts[:, :, 2], axis=0)
    rows = jnp.concatenate(
        [jnp.where(xi == 0, summed, rows[:, :TILE]), rows[:, TILE:], summed], axis=1
    )
    rows = copies(rows, "z", nz).reshape(2 * nz, -1)

    made = jnp.stack(
        [
            jnp.stack([product(b[-j % nx], slab) for b, slab in ((block0, slab0), (block1, slab1))])
            for j in range(nx)
        ]
    )
    made = (made * SCALE).astype(jnp.float16).reshape(nx, 2, 2, TILE, 2 * TILE)
    made = jnp.stack(
        [
            lax.dynamic_index_in_dim(made, lax.rem(r - xi + nx, nx), 0, keepdims=False)
            for r in range(ny)
        ]
    )
    picked = exchanged(made, "y")

    near = copies(after(rows, picked), "y", ny).reshape(count, -1)
    far = shifted(near, "c", nc, 1)

    def in_order(value):
        value = value.reshape(nc, ny * nz, 2, -1)
        value = jnp.where(ci == 0, value, value[::-1])
        return value.transpose(1, 0, 2, 3).reshape(TILE, -1)

    def as_lies(value):
        value = value.reshape(ny * nz, nc, 2, -1).transpose(1, 0, 2, 3)
        value = jnp.where(ci == 0, value, value[::-1])
        return value.reshape(TILE, -1)

    edge = per_range * TILE
    own = lax.dynamic_slice_in_dim(near, lax.rem(here - ci, 16) * 2 * TILE, 4 * TILE, 1)
    own = lax.dynamic_index_in_dim(copies(own, "x", nx), yi, 0, keepdims=False)
    own, others = (own[:, : 2 * TILE], own[:, 2 * TILE :])
    own, others = jnp.where(ci == 0, own, others), jnp.where(ci == 0, others, own)
    own = jnp.concatenate([own, shifted(others, "c", nc, 1)], axis=0)

    def hop(low, high):
        return shifted(low, "z", nz, 1), shifted(high, "z", nz, -1)

    low1, high1 = hop(picked, picked)
    low2, high2 = hop(low1, high1)
    corner = in_order(jnp.concatenate([near[:, edge:], far[:, edge:]], axis=0))
    upper, inverse = factored(after(corner, low1, high1))
    low2, high2 = lax.optimization_barrier((low2, high2, far, upper))[:2]
    low3, high3 = hop(low2, high2)
    bulk = [picked, low1, low2, low3, None, high3, high2, high1]

    names = names.reshape(nz, ny * nc * 16)
    names = jnp.take(names, lax.rem(zi - jnp.arange(nz) + nz, nz), axis=0).reshape(count, 16)
    in_range = entry % 8 // 2 == yi
    owner = jnp.floor(names * 0.5)
    first_half = entry < 8

    def scattered(owned):
        match = in_range & (owner == owned)
        hits = [
            jnp.sum(jnp.where(match & half, 1.0, 0.0), axis=1, keepdims=True)
            for half in (first_half, ~first_half)
        ]
        return match, hits

    match, hits = scattered(here.astype(f32))
    hit = jnp.where(first_half, hits[0], hits[1])
    fields = [
        (hits[0] + hits[1])[:, 0],
        jnp.sum(jnp.where(match, names - 2.0 * owner, 0.0), axis=1),
        jnp.sum(jnp.where(entry % 8 == xi * 2, hit * (names - xi * per_range), 0.0), axis=1),
        jnp.sum(jnp.where(entry % 8 == xi * 2 + 1, hit * (names - xi * per_range), 0.0), axis=1),
    ]
    fields = jnp.stack(fields).astype(jnp.int32).reshape(4, nz, ny, nc).transpose(0, 3, 1, 2)
    fields = jnp.where(ci == 0, fields, fields[:, ::-1])

    def flags(match):
        match = match.reshape(nz, ny, nc, 2, 8)
        match = lax.dynamic_index_in_dim(match, ci, 2, keepdims=False)
        return lax.dynamic_slice_in_dim(match, yi * 2, 2, 3).transpose(2, 3, 0, 1)

    to_me = flags(match)
    to_other = flags(scattered((here + 1 - 2 * ci).astype(f32))[0])

    def choose(k, match):
        def flag(s, t):
            return match[s, t, k][:, None, None]

        return pick_slot(bulk[k], flag)

    def pick_slot(got, flag):
        second = jnp.where(flag(1, 0), got[:, 1, 0], got[:, 1, 1])
        return jnp.where(flag(0, 0), got[:, 0, 0], jnp.where(flag(0, 1), got[:, 0, 1], second))

    def batch(ks):
        mine = jnp.concatenate([choose(k, to_me) for k in ks], axis=0)
        other = jnp.concatenate([choose(k, to_other) for k in ks], axis=0)
        both = jnp.concatenate([mine, shifted(other, "c", nc, 1)], axis=0)
        table = jnp.concatenate([fields[:, :, k] for k in ks], axis=2)
        return table.reshape(4, -1), both.astype(f32) * (1.0 / SCALE)

    first_table, first_tiles = batch((0, 1, 7, 2, 6))
    solved = jnp.dot(inverse, in_order(own), precision=HIGH, preferred_element_type=f32)
    solved = jnp.concatenate(
        [jnp.where(here == 0, upper, solved[:, :TILE]), solved[:, TILE:]], axis=1
    )
    panel = solved.T
    weight = as_lies(jnp.dot(inverse.T, solved, precision=HIGH, preferred_element_type=f32)).T
    low, high = lax.optimization_barrier((bulk[3], bulk[5], weight, first_tiles))[:2]
    bulk[3], bulk[5] = low, high
    half = low.shape[0] // 2
    opposite = jnp.concatenate(
        [shifted(low[:half], "z", nz, 1), shifted(high[half:], "z", nz, -1)],
        axis=0,
    )
    place = (here * 2 - xi * per_range).astype(jnp.int32)[None]
    shape = (2 * TILE, per_range * TILE)
    start = first_sum(first_table, place, weight, near, far, first_diag, first_tiles, shape)
    late = [batch((3, 5))]
    bulk[4] = after(opposite, start)
    late.append(batch((4,)))
    last_table = jnp.concatenate([e[0] for e in late], axis=1)
    last_tiles = jnp.concatenate([e[1] for e in late], axis=0)
    return panel, second_sum(last_table, start, last_tiles)


def solution(mesh):
    grid = Mesh(mesh.devices.reshape(4, 8, 2, 4), ("y", "z", "c", "x"))
    scen = ("y", "z", "c")
    in_specs = (P(scen, None, None), P(scen, None, "x"), P(scen, None), P(scen, None))
    out_specs = (P(scen, None), P(scen, "x"))

    return jax.shard_map(
        per_device, mesh=grid, in_specs=in_specs, out_specs=out_specs, check_vma=False
    )
```
